32 devices in a mesh: cell: 4 (over y, x), chan: 8 (over z, core).
Axes of the slice: x: 2, y: 2, z: 4, core: 2. Of those that a mesh axis runs over, the one named last changes fastest.
Arguments:
- slab: bfloat16 [32768, 8192], P('cell', 'chan'), may hold values from -6 to 6
- cell_factor: float32 [32, 32768], P(None, 'cell'), may hold values from -6 to 6
- chan_factor: float32 [32, 8192], P(None, 'chan'), may hold values from -6 to 6
- cell_mttkrp: float32 [32, 32768], P(None, 'cell'), may hold values from -12 to 12
- chan_mttkrp: float32 [32, 8192], P(None, 'chan'), may hold values from -12 to 12
- cell_gram_acc: float32 [32, 32], replicated, as said below
- chan_gram_acc: float32 [32, 32], replicated, as said below
Outputs:
- time_row: float32 [32], replicated
- new_cell_factor: float32 [32, 32768], P(None, 'cell')
- new_chan_factor: float32 [32, 8192], P(None, 'chan')
- new_cell_mttkrp: float32 [32, 32768], P(None, 'cell')
- new_chan_mttkrp: float32 [32, 8192], P(None, 'chan')
- new_cell_gram: float32 [32, 32], replicated
- new_chan_gram: float32 [32, 32], replicated
The draws below stay inside these ranges and needn't reach their ends.
Inputs may be any that keep to these rules, and one draw needn't show every extreme that they name: `cell_gram_acc`: symmetric with a dominant positive diagonal. `chan_gram_acc`: symmetric with a dominant positive diagonal.
All inputs are finite; a program needn't handle non-finite values.
Results may differ from the reference program's by a relative error of at most 0.0033.
Values sent between devices are 32-bit elements; how exact they have to be, the bound alone decides.
No kernel may reach another device: no remote copies, remote signals or barrier semaphores. Data moves between devices by JAX's collectives and lax.ppermute only.
A program may use at most 64 MiB of HBM per device.

```python
import math
import jax
import jax.numpy as jnp
from jax import lax

RANK = 32
CHANNELS = 8192
CELLS = 32768


def dominant_gram(key):
    diag_key = jax.random.fold_in(key, 11)
    off_key = jax.random.fold_in(key, 23)
    diag = jax.random.uniform(diag_key, (RANK,), jnp.float32, 3.0, 6.0)
    off = jax.random.uniform(off_key, (RANK, RANK), jnp.float32, -0.06, 0.06)
    sym = 0.5 * (off + off.T)
    eye = jnp.eye(RANK, dtype=jnp.float32)
    return sym * (1.0 - eye) + eye * diag[None, :]


def draw_cell_gram_acc(key, part):
    return dominant_gram(jax.random.fold_in(key, 101))


def draw_chan_gram_acc(key, part):
    return dominant_gram(jax.random.fold_in(key, 202))


def block_levels(key, extent, pieces, smallest, largest):
    gain = 1.0
    for position, blocks in pieces:
        draws = jax.random.uniform(jax.random.fold_in(jax.random.fold_in(key, 6), position), (blocks,), jnp.float32, smallest / len(pieces), largest / len(pieces))
        gain = gain * jnp.repeat(jnp.exp(draws), extent[position] // blocks).reshape((-1,) + (1,) * (len(extent) - 1 - position))
    return gain


def noise(stream_key, extent, deviation, reach, pieces=(), kind=jnp.bfloat16):
    entries = jax.random.normal(stream_key, extent, jnp.float32) * deviation
    if len(pieces) > 0:
        entries = block_levels(stream_key, extent, pieces, -0.22, 0.18) * entries
    return jnp.clip(entries, min=-reach, max=reach).astype(kind)


def setup_inputs(seed: int = 0) -> dict:
    streams_of = jax.random.split(jax.random.key(seed), 8)
    slab = noise(streams_of[0], (CELLS, CHANNELS), 1.0, 6.0, ((0, 4), (1, 8)))
    cell_factor = noise(streams_of[1], (RANK, CELLS), 1.0, 6.0, ((1, 4),), jnp.float32)
    chan_factor = noise(streams_of[2], (RANK, CHANNELS), 1.0, 6.0, ((1, 8),), jnp.float32)
    cell_mttkrp = noise(streams_of[3], (RANK, CELLS), 2.0, 12.0, ((1, 4),), jnp.float32)
    chan_mttkrp = noise(streams_of[4], (RANK, CHANNELS), 2.0, 12.0, ((1, 8),), jnp.float32)
    cell_gram_acc = draw_cell_gram_acc(jax.random.fold_in(streams_of[7], 71), 0)
    chan_gram_acc = draw_chan_gram_acc(jax.random.fold_in(streams_of[7], 71), 0)
    return dict(slab=slab, cell_factor=cell_factor, chan_factor=chan_factor, cell_mttkrp=cell_mttkrp, chan_mttkrp=chan_mttkrp, cell_gram_acc=cell_gram_acc, chan_gram_acc=chan_gram_acc)


def spd_solve(matrix, right):
    lower = jnp.linalg.cholesky(matrix)
    return jax.scipy.linalg.cho_solve((lower, True), right)

def reference(slab, cell_factor, chan_factor, cell_mttkrp, chan_mttkrp, cell_gram_acc, chan_gram_acc):
    hi = lax.Precision.HIGHEST
    chan_low = chan_factor.astype(jnp.bfloat16)
    slab_chan = lax.dot_general(chan_low.astype(jnp.float32), slab.astype(jnp.float32), (((1,), (1,)), ((), ())), preferred_element_type=jnp.float32)
    rhs = lax.optimization_barrier(jnp.sum(cell_factor * slab_chan, axis=1)) / math.sqrt(CELLS * CHANNELS)
    cell_norm = jnp.dot(cell_factor, cell_factor.T, precision=hi) / CELLS
    chan_norm = jnp.dot(chan_factor, chan_factor.T, precision=hi) / CHANNELS
    time_row = spd_solve(cell_norm * chan_norm, rhs[:, None])[:, 0]
    outer = time_row[:, None] * time_row[None, :]
    new_cell_mttkrp = cell_mttkrp + time_row[:, None] * slab_chan / math.sqrt(CHANNELS)
    new_cell_gram = cell_gram_acc + chan_norm * outer
    new_cell_factor = spd_solve(new_cell_gram, new_cell_mttkrp)
    new_norm = jnp.dot(new_cell_factor, new_cell_factor.T, precision=hi) / CELLS
    cell_low = new_cell_factor.astype(jnp.bfloat16)
    slab_cell = jnp.dot(cell_low.astype(jnp.float32), slab.astype(jnp.float32), preferred_element_type=jnp.float32)
    new_chan_mttkrp = chan_mttkrp + time_row[:, None] * slab_cell / math.sqrt(CELLS)
    new_chan_gram = chan_gram_acc + new_norm * outer
    new_chan_factor = spd_solve(new_chan_gram, new_chan_mttkrp)
    return (time_row, new_cell_factor, new_chan_factor, new_cell_mttkrp, new_chan_mttkrp, new_cell_gram, new_chan_gram)
```

```python
import functools
import math

import jax
import jax.numpy as jnp
from jax import lax
from jax.experimental import pallas as pl
from jax.experimental.pallas import tpu as pltpu
from jax.sharding import PartitionSpec as P

CHUNKS = 4
STATS_CHUNK = 1
LANES = 128
HI = lax.Precision.HIGHEST
ROWS = (((1,), (1,)), ((), ()))
WHOLE = pl.BlockSpec(memory_space=pltpu.VMEM)
PARAMS = pltpu.CompilerParams(vmem_limit_bytes=44 << 20)


def eye(n):
    i = lax.broadcasted_iota(jnp.int32, (n, n), 0)
    j = lax.broadcasted_iota(jnp.int32, (n, n), 1)
    return (i == j).astype(jnp.float32)


def eliminate(aug, n):
    rows = lax.broadcasted_iota(jnp.int32, aug.shape, 0)
    for k in range(n):
        row = aug[k : k + 1, :] * (1.0 / aug[k : k + 1, k : k + 1])
        aug = jnp.where(rows == k, row, aug - aug[:, k : k + 1] * row)
    return aug[:, n:]


def pass_one(all_rows, all_cols, n_cell, n_chan, chan_ref, cell_ref, slab_ref, *refs):
    sends, keeps = refs[:CHUNKS], refs[CHUNKS : 2 * CHUNKS]
    stats_ref, slab_v, sem = refs[2 * CHUNKS :]
    core = lax.rem(lax.axis_index("chan"), 2)
    width = slab_ref.shape[0] // (2 * CHUNKS)
    jobs = []
    for k in range(CHUNKS):
        for half, out in ((1 - core, sends[k]), (core, keeps[k])):
            at = pl.ds(pl.multiple_of((2 * k + half) * width, width), width)
            copy = pltpu.make_async_copy(slab_ref.at[at], slab_v.at[at], sem.at[len(jobs)])
            copy.start()
            jobs.append((copy, at, out))
    chan = chan_ref[...]
    low = chan.astype(jnp.bfloat16)
    cell = cell_ref[...]
    chan_gram = lax.dot_general(chan, chan, ROWS, precision=HI) / (all_cols * n_cell)
    cell_gram = lax.dot_general(cell, cell, ROWS, precision=HI) / (all_rows * n_chan)
    total = jnp.zeros((chan.shape[0], LANES), jnp.float32)
    for copy, at, out in jobs:
        copy.wait()
        part = lax.dot_general(low, slab_v[at], ROWS, preferred_element_type=jnp.float32)
        out[...] = part
        part = part * cell_ref[:, at]
        for j in range(0, width, LANES):
            total += part[:, j : j + LANES]
    rhs = jnp.sum(total, axis=1, keepdims=True) / math.sqrt(all_rows * all_cols)
    pad = jnp.zeros((chan.shape[0], LANES - 1 - 2 * chan.shape[0]), jnp.float32)
    stats_ref[...] = jnp.concatenate([cell_gram, chan_gram, rhs, pad], axis=1)


def solve_one(stats_ref, acc_ref, row_ref, gram_ref, out_ref):
    stats = stats_ref[...]
    n = stats.shape[0]
    cell_norm, chan_norm, rhs = stats[:, :n], stats[:, n : 2 * n], stats[:, 2 * n : 2 * n + 1]
    time = eliminate(jnp.concatenate([cell_norm * chan_norm, rhs], axis=1), n)
    row = jnp.sum(eye(n) * time, axis=0, keepdims=True)
    outer = time * row
    gram = acc_ref[...] + chan_norm * outer
    inverse = eliminate(jnp.concatenate([gram, eye(n)], axis=1), n)
    row_ref[...] = row
    gram_ref[...] = gram
    pad = jnp.zeros((n, LANES - 2 * n - 1), jnp.float32)
    out_ref[...] = jnp.concatenate([inverse, outer, time, pad], axis=1)


def pass_two(all_rows, all_cols, solved_ref, mttkrp_ref, slab_v, *refs):
    own, other = refs[:CHUNKS], refs[CHUNKS : 2 * CHUNKS]
    new_mttkrp, new_factor, out_ref = refs[2 * CHUNKS :]
    n = solved_ref.shape[0]
    core = lax.rem(lax.axis_index("chan"), 2)
    width = slab_v.shape[0] // (2 * CHUNKS)
    cols = slab_v.shape[1]
    inverse = solved_ref[:, :n]
    time = solved_ref[:, 2 * n : 2 * n + 1] / math.sqrt(all_cols)
    total = jnp.zeros((n, cols), jnp.float32)
    gram = jnp.zeros((n, n), jnp.float32)
    for k in range(CHUNKS):
        for half, part in ((core, own[k]), (1 - core, other[k])):
            at = pl.ds(pl.multiple_of((2 * k + half) * width, width), width)
            right = mttkrp_ref[:, at] + time * part[:, :width]
            new_mttkrp[:, at] = right
            factor = jnp.dot(inverse, right, precision=HI)
            new_factor[:, at] = factor
            gram += lax.dot_general(factor, factor, ROWS, precision=HI)
            low = factor.astype(jnp.bfloat16)
            total += jnp.dot(low, slab_v[at], preferred_element_type=jnp.float32)
    out_ref[:, :cols] = total
    pad = jnp.zeros((n, LANES - n), jnp.float32)
    out_ref[:, cols:] = jnp.concatenate([gram / all_rows, pad], axis=1)


def solve_two(all_rows, n_parts, solved_ref, mttkrp_ref, acc_ref, *refs):
    parts = [r[...] for r in refs[:n_parts]]
    new_mttkrp, new_factor, new_gram = refs[n_parts:]
    while len(parts) > 1:
        parts = [a + b for a, b in zip(parts[::2], parts[1::2])]
    (summed,) = parts
    n, cols = mttkrp_ref.shape
    outer = solved_ref[:, n : 2 * n]
    time = solved_ref[:, 2 * n : 2 * n + 1] / math.sqrt(all_rows)
    gram = acc_ref[...] + summed[:, cols : cols + n] * outer
    inverse = eliminate(jnp.concatenate([gram, eye(n)], axis=1), n)
    right = mttkrp_ref[...] + time * summed[:, :cols]
    new_mttkrp[...] = right
    new_factor[...] = jnp.dot(inverse, right, precision=HI)
    new_gram[...] = gram


def over_cell(x, n_cell):
    masks = 1
    while masks < n_cell // 4:
        masks *= 2
        x = x + lax.ppermute(x, "cell", [(i, i ^ (2 * masks)) for i in range(n_cell)])
    near = [m for m in (1, 2, 3) if m < n_cell]
    return [x] + [lax.ppermute(x, "cell", [(i, i ^ m) for i in range(n_cell)]) for m in near]


def pair_sum(parts):
    while len(parts) > 1:
        parts = [a + b for a, b in zip(parts[::2], parts[1::2])]
    return parts[0]


def hop(x, moves):
    return lax.ppermute(x, "chan", [(2 * a + c, 2 * b + c) for a, b in moves for c in (0, 1)])


def over_chips(x, n_chip):
    chip = lax.axis_index("chan") // 2
    far = n_chip - 1
    half = n_chip // 2
    for s in range(half - 1):
        x = x + hop(x, [(s, s + 1), (far - s, far - s - 1)])
    x = x + hop(x, [(half - 1, half), (half, half - 1)])
    for s in reversed(range(half - 1)):
        got = hop(x, [(s + 1, s), (far - s - 1, far - s)])
        x = jnp.where((chip == s) | (chip == far - s), got, x)
    return x


def body(slab, cell_factor, chan_factor, cell_mttkrp, chan_mttkrp, cell_gram_acc, chan_gram_acc):
    n_cell = lax.axis_size("cell")
    n_chan = lax.axis_size("chan")
    rows, cols = slab.shape
    rank = cell_factor.shape[0]
    all_rows, all_cols = rows * n_cell, cols * n_chan
    width = rows // (2 * CHUNKS)
    f32 = functools.partial(jax.ShapeDtypeStruct, dtype=jnp.float32)

    first = pl.pallas_call(
        functools.partial(pass_one, all_rows, all_cols, n_cell, n_chan),
        in_specs=[WHOLE, WHOLE, pl.BlockSpec(memory_space=pl.ANY)],
        out_specs=[WHOLE] * (2 * CHUNKS + 2),
        out_shape=[f32((rank, width))] * (2 * CHUNKS)
        + [f32((rank, LANES)), pltpu.VMEM((rows, cols), slab.dtype)],
        scratch_shapes=[pltpu.SemaphoreType.DMA((2 * CHUNKS,))],
        compiler_params=PARAMS,
        name="pass_one",
    )(chan_factor, cell_factor, slab)
    sends, keeps = list(first[:CHUNKS]), list(first[CHUNKS : 2 * CHUNKS])
    stats, slab_v = first[2 * CHUNKS :]
    slab_v = pltpu.with_memory_space_constraint(slab_v, pltpu.VMEM)

    stats = pair_sum(over_cell(stats, n_cell))
    sends[STATS_CHUNK] = jnp.concatenate([sends[STATS_CHUNK], stats], axis=1)
    keeps[STATS_CHUNK] = jnp.concatenate([keeps[STATS_CHUNK], stats], axis=1)
    swap = [(i, i ^ 1) for i in range(n_chan)]
    own = [keep + lax.ppermute(send, "chan", swap) for send, keep in zip(sends, keeps)]
    own = [over_chips(x, n_chan // 2) for x in own]
    other = [lax.ppermute(x[:, :width], "chan", swap) for x in own]

    row, new_cell_gram, solved = pl.pallas_call(
        solve_one,
        in_specs=[WHOLE] * 2,
        out_specs=[WHOLE] * 3,
        out_shape=[f32((1, rank)), f32((rank, rank)), f32((rank, LANES))],
        name="solve_one",
    )(own[STATS_CHUNK][:, width:], cell_gram_acc)

    new_cell_mttkrp, new_cell_factor, part = pl.pallas_call(
        functools.partial(pass_two, all_rows, all_cols),
        in_specs=[WHOLE] * (3 + 2 * CHUNKS),
        out_specs=[WHOLE] * 3,
        out_shape=[f32((rank, rows)), f32((rank, rows)), f32((rank, cols + LANES))],
        compiler_params=PARAMS,
        name="pass_two",
    )(solved, cell_mttkrp, slab_v, *own, *other)

    parts = over_cell(part, n_cell)
    new_chan_mttkrp, new_chan_factor, new_chan_gram = pl.pallas_call(
        functools.partial(solve_two, all_rows, len(parts)),
        in_specs=[WHOLE] * (3 + len(parts)),
        out_specs=[WHOLE] * 3,
        out_shape=[f32((rank, cols)), f32((rank, cols)), f32((rank, rank))],
        name="solve_two",
    )(solved, chan_mttkrp, chan_gram_acc, *parts)
    return (
        row.reshape(rank),
        new_cell_factor,
        new_chan_factor,
        new_cell_mttkrp,
        new_chan_mttkrp,
        new_cell_gram,
        new_chan_gram,
    )


def solution(mesh):
    placed = (
        P("cell", "chan"),
        P(None, "cell"),
        P(None, "chan"),
        P(None, "cell"),
        P(None, "chan"),
        P(),
        P(),
    )
    return jax.shard_map(
        body,
        mesh=mesh,
        in_specs=placed,
        out_specs=(
            P(),
            P(None, "cell"),
            P(None, "chan"),
            P(None, "cell"),
            P(None, "chan"),
            P(),
            P(),
        ),
        check_vma=False,
    )
```

```python
import functools
import math

import jax
import jax.numpy as jnp
from jax import lax
from jax.experimental import pallas as pl
from jax.experimental.pallas import tpu as pltpu
from jax.sharding import PartitionSpec as P

CHUNKS = 2
STATS_CHUNK = 1
LANES = 128
HI = lax.Precision.HIGHEST
ROWS = (((1,), (1,)), ((), ()))
WHOLE = pl.BlockSpec(memory_space=pltpu.VMEM)
PARAMS = pltpu.CompilerParams(vmem_limit_bytes=12 << 20)
SMALL = pltpu.CompilerParams(vmem_limit_bytes=4 << 20)


def eye(n):
    i = lax.broadcasted_iota(jnp.int32, (n, n), 0)
    j = lax.broadcasted_iota(jnp.int32, (n, n), 1)
    return (i == j).astype(jnp.float32)


def eliminate(aug, n):
    rows = lax.broadcasted_iota(jnp.int32, aug.shape, 0)
    for k in range(n):
        row = aug[k : k + 1, :] * (1.0 / aug[k : k + 1, k : k + 1])
        aug = jnp.where(rows == k, row, aug - aug[:, k : k + 1] * row)
    return aug[:, n:]


def place(block, rel, n_rel, width):
    me = lax.rem(lax.axis_index("chan"), n_rel)
    at = (block * n_rel + lax.bitwise_xor(me, rel)) * width
    return pl.ds(pl.multiple_of(at, width), width)


def pass_one(all_rows, all_cols, n_cell, n_chan, chan_hbm, cell_hbm, slab_hbm, *refs):
    sends, keeps = refs[:CHUNKS], refs[CHUNKS : 2 * CHUNKS]
    stats_ref, slab_v, chan_ref, cell_ref, sem, small_sem = refs[2 * CHUNKS :]
    n_rel = n_chan // 2
    width = slab_hbm.shape[0] // (CHUNKS * n_rel)
    chan_copy = pltpu.make_async_copy(chan_hbm, chan_ref, small_sem.at[0])
    cell_copy = pltpu.make_async_copy(cell_hbm, cell_ref, small_sem.at[1])
    chan_copy.start()
    jobs = []
    for k in range(CHUNKS):
        for rel in [*range(1, n_rel, 2), *range(0, n_rel, 2)]:
            at = place(k, rel, n_rel, width)
            copy = pltpu.make_async_copy(slab_hbm.at[at], slab_v.at[at], sem.at[len(jobs)])
            copy.start()
            if not jobs:
                cell_copy.start()
            out = (sends if rel % 2 else keeps)[k]
            jobs.append((copy, at, out.at[:, pl.ds(rel // 2 * width, width)]))
    chan_copy.wait()
    chan = chan_ref[...]
    low = chan.astype(jnp.bfloat16)
    chan_gram = lax.dot_general(chan, chan, ROWS, precision=HI) / (all_cols * n_cell)
    cell_copy.wait()
    cell = cell_ref[...]
    cell_gram = lax.dot_general(cell, cell, ROWS, precision=HI) / (all_rows * n_chan)
    total = jnp.zeros((chan.shape[0], LANES), jnp.float32)
    for copy, at, out in jobs:
        copy.wait()
        part = lax.dot_general(low, slab_v[at], ROWS, preferred_element_type=jnp.float32)
        out[...] = part
        part = part * cell_ref[:, at]
        for j in range(0, width, LANES):
            total += part[:, j : j + LANES]
    rhs = jnp.sum(total, axis=1, keepdims=True) / math.sqrt(all_rows * all_cols)
    pad = jnp.zeros((chan.shape[0], LANES - 1 - 2 * chan.shape[0]), jnp.float32)
    stats_ref[...] = jnp.concatenate([cell_gram, chan_gram, rhs, pad], axis=1)


def solve_one(stats_ref, acc_ref, row_ref, gram_ref, out_ref):
    stats = stats_ref[...]
    n = stats.shape[0]
    cell_norm, chan_norm, rhs = stats[:, :n], stats[:, n : 2 * n], stats[:, 2 * n : 2 * n + 1]
    time = eliminate(jnp.concatenate([cell_norm * chan_norm, rhs], axis=1), n)
    row = jnp.sum(eye(n) * time, axis=0, keepdims=True)
    outer = time * row
    gram = acc_ref[...] + chan_norm * outer
    inverse = eliminate(jnp.concatenate([gram, eye(n)], axis=1), n)
    row_ref[...] = row
    gram_ref[...] = gram
    pad = jnp.zeros((n, LANES - 2 * n - 1), jnp.float32)
    out_ref[...] = jnp.concatenate([inverse, outer, time, pad], axis=1)


def pass_two(all_rows, all_cols, where, n_rel, solved_ref, mttkrp_ref, slab_v, *refs):
    pieces = refs[: len(where)]
    new_mttkrp, new_factor, out_ref = refs[len(where) :]
    n = solved_ref.shape[0]
    cols = slab_v.shape[1]
    inverse = solved_ref[:, :n]
    time = solved_ref[:, 2 * n : 2 * n + 1] / math.sqrt(all_cols)
    total = jnp.zeros((n, cols), jnp.float32)
    gram = jnp.zeros((n, n), jnp.float32)
    for (chunk, rel), piece in zip(where, pieces):
        width = piece.shape[1]
        at = place(chunk, rel, n_rel, width)
        right = mttkrp_ref[:, at] + time * piece[...]
        new_mttkrp[:, at] = right
        factor = jnp.dot(inverse, right, precision=HI)
        new_factor[:, at] = factor
        gram += lax.dot_general(factor, factor, ROWS, precision=HI)
        low = factor.astype(jnp.bfloat16)
        total += jnp.dot(low, slab_v[at], preferred_element_type=jnp.float32)
    out_ref[:, :cols] = total
    pad = jnp.zeros((n, LANES - n), jnp.float32)
    out_ref[:, cols:] = jnp.concatenate([gram / all_rows, pad], axis=1)


def solve_two(all_rows, n_parts, solved_ref, mttkrp_ref, acc_ref, *refs):
    parts = [r[...] for r in refs[:n_parts]]
    new_mttkrp, new_factor, new_gram = refs[n_parts:]
    while len(parts) > 1:
        parts = [a + b for a, b in zip(parts[::2], parts[1::2])]
    (summed,) = parts
    n, cols = mttkrp_ref.shape
    outer = solved_ref[:, n : 2 * n]
    time = solved_ref[:, 2 * n : 2 * n + 1] / math.sqrt(all_rows)
    gram = acc_ref[...] + summed[:, cols : cols + n] * outer
    inverse = eliminate(jnp.concatenate([gram, eye(n)], axis=1), n)
    right = mttkrp_ref[...] + time * summed[:, :cols]
    new_mttkrp[...] = right
    new_factor[...] = jnp.dot(inverse, right, precision=HI)
    new_gram[...] = gram


def over_cell(x, n_cell):
    masks = 1
    while masks < n_cell // 4:
        masks *= 2
        x = x + lax.ppermute(x, "cell", [(i, i ^ (2 * masks)) for i in range(n_cell)])
    near = [m for m in (1, 2, 3) if m < n_cell]
    return [x] + [lax.ppermute(x, "cell", [(i, i ^ m) for i in range(n_cell)]) for m in near]


def pair_sum(parts):
    while len(parts) > 1:
        parts = [a + b for a, b in zip(parts[::2], parts[1::2])]
    return parts[0]


def trade(x, mask, n_chan):
    return lax.ppermute(x, "chan", [(i, i ^ mask) for i in range(n_chan)])


def over_chan(send, keep, extra, n_chan):
    width = keep.shape[1] // (n_chan // 4)
    if extra is not None:
        send = jnp.concatenate([send, extra], axis=1)
        keep = jnp.concatenate([keep, extra], axis=1)
    size = keep.shape[1] - (0 if extra is None else LANES)
    mask = 1
    while True:
        x = keep + trade(send, mask, n_chan)
        mask *= 2
        if mask == n_chan // 2:
            break
        blocks = [x[:, i * width : (i + 1) * width] for i in range(size // width)]
        tail = [] if extra is None else [x[:, size:]]
        keep = jnp.concatenate(blocks[::2] + tail, axis=1) if len(blocks) > 2 or tail else blocks[0]
        send = jnp.concatenate(blocks[1::2] + tail, axis=1) if len(blocks) > 2 or tail else blocks[1]
        size //= 2
    x = x + trade(x, mask, n_chan)
    have = {0: x[:, :width]}
    while mask > 1:
        mask //= 2
        have.update({rel + mask: trade(block, mask, n_chan) for rel, block in list(have.items())})
    return have, None if extra is None else x[:, width:]


def body(slab, cell_factor, chan_factor, cell_mttkrp, chan_mttkrp, cell_gram_acc, chan_gram_acc):
    n_cell = lax.axis_size("cell")
    n_chan = lax.axis_size("chan")
    rows, cols = slab.shape
    rank = cell_factor.shape[0]
    all_rows, all_cols = rows * n_cell, cols * n_chan
    n_rel = n_chan // 2
    width = rows // (CHUNKS * n_rel)
    f32 = functools.partial(jax.ShapeDtypeStruct, dtype=jnp.float32)

    first = pl.pallas_call(
        functools.partial(pass_one, all_rows, all_cols, n_cell, n_chan),
        in_specs=[pl.BlockSpec(memory_space=pltpu.HBM)] * 3,
        out_specs=[WHOLE] * (2 * CHUNKS + 2),
        out_shape=[f32((rank, width * n_rel // 2))] * (2 * CHUNKS)
        + [f32((rank, LANES)), pltpu.VMEM((rows, cols), slab.dtype)],
        scratch_shapes=[
            pltpu.VMEM(chan_factor.shape, jnp.float32),
            pltpu.VMEM(cell_factor.shape, jnp.float32),
            pltpu.SemaphoreType.DMA((CHUNKS * n_rel,)),
            pltpu.SemaphoreType.DMA((2,)),
        ],
        compiler_params=PARAMS,
        name="pass_one",
    )(*(pltpu.with_memory_space_constraint(x, pltpu.HBM) for x in (chan_factor, cell_factor, slab)))
    sends, keeps = list(first[:CHUNKS]), list(first[CHUNKS : 2 * CHUNKS])
    stats, slab_v = first[2 * CHUNKS :]
    slab_v = pltpu.with_memory_space_constraint(slab_v, pltpu.VMEM)

    stats = pair_sum(over_cell(stats, n_cell))
    where, pieces = [], []
    for k in range(CHUNKS):
        have, got = over_chan(sends[k], keeps[k], stats if k == STATS_CHUNK else None, n_chan)
        where += [(k, rel) for rel in have]
        pieces += have.values()
        if got is not None:
            summed = got

    row, new_cell_gram, solved = pl.pallas_call(
        solve_one,
        in_specs=[WHOLE] * 2,
        out_specs=[WHOLE] * 3,
        out_shape=[f32((1, rank)), f32((rank, rank)), f32((rank, LANES))],
        compiler_params=SMALL,
        name="solve_one",
    )(summed, cell_gram_acc)

    new_cell_mttkrp, new_cell_factor, part = pl.pallas_call(
        functools.partial(pass_two, all_rows, all_cols, where, n_rel),
        in_specs=[WHOLE] * (3 + len(where)),
        out_specs=[WHOLE] * 3,
        out_shape=[f32((rank, rows)), f32((rank, rows)), f32((rank, cols + LANES))],
        compiler_params=PARAMS,
        name="pass_two",
    )(solved, cell_mttkrp, slab_v, *pieces)

    parts = over_cell(part, n_cell)
    new_chan_mttkrp, new_chan_factor, new_chan_gram = pl.pallas_call(
        functools.partial(solve_two, all_rows, len(parts)),
        in_specs=[WHOLE] * (3 + len(parts)),
        out_specs=[WHOLE] * 3,
        out_shape=[f32((rank, cols)), f32((rank, cols)), f32((rank, rank))],
        compiler_params=SMALL,
        name="solve_two",
    )(solved, chan_mttkrp, chan_gram_acc, *parts)
    return (
        row.reshape(rank),
        new_cell_factor,
        new_chan_factor,
        new_cell_mttkrp,
        new_chan_mttkrp,
        new_cell_gram,
        new_chan_gram,
    )


def solution(mesh):
    placed = (
        P("cell", "chan"),
        P(None, "cell"),
        P(None, "chan"),
        P(None, "cell"),
        P(None, "chan"),
        P(),
        P(),
    )
    return jax.shard_map(
        body,
        mesh=mesh,
        in_specs=placed,
        out_specs=(
            P(),
            P(None, "cell"),
            P(None, "chan"),
            P(None, "cell"),
            P(None, "chan"),
            P(),
            P(),
        ),
        check_vma=False,
    )
```

```python
import functools
import math

import jax
import jax.numpy as jnp
from jax import lax
from jax.experimental import pallas as pl
from jax.experimental.pallas import tpu as pltpu
from jax.sharding import PartitionSpec as P

CHUNKS = 2
LANES = 128
HI = lax.Precision.HIGHEST
ROWS = (((1,), (1,)), ((), ()))
WHOLE = pl.BlockSpec(memory_space=pltpu.VMEM)
PARAMS = pltpu.CompilerParams(vmem_limit_bytes=12 << 20)


def cost(us):
    return pl.CostEstimate(flops=int(us * 1e9), bytes_accessed=int(us * 3e6), transcendentals=0)


SMALL = pltpu.CompilerParams(vmem_limit_bytes=4 << 20)


def eye(n):
    i = lax.broadcasted_iota(jnp.int32, (n, n), 0)
    j = lax.broadcasted_iota(jnp.int32, (n, n), 1)
    return (i == j).astype(jnp.float32)


def eliminate(aug, n):
    rows = lax.broadcasted_iota(jnp.int32, aug.shape, 0)
    for k in range(n):
        row = aug[k : k + 1, :] * (1.0 / aug[k : k + 1, k : k + 1])
        aug = jnp.where(rows == k, row, aug - aug[:, k : k + 1] * row)
    return aug[:, n:]


def place(rel, n_rel, width):
    me = lax.rem(lax.axis_index("chan"), n_rel)
    return pl.multiple_of(lax.bitwise_xor(me, rel) * width, width)


def multiply(start, n_rel, low_ref, cell_ref, slab_hbm, slab_v, sem, send_ref, keep_ref, load):
    width = slab_v.shape[0] // n_rel
    jobs = []
    for rel in [*range(1, n_rel, 2), *range(0, n_rel, 2)]:
        at = place(rel, n_rel, width)
        rows = pl.ds(pl.multiple_of(start + at, width), width)
        here = pl.ds(at, width)
        copy = pltpu.make_async_copy(slab_hbm.at[rows], slab_v.at[here], sem.at[len(jobs)])
        copy.start()
        out = (send_ref if rel % 2 else keep_ref).at[:, pl.ds(rel // 2 * width, width)]
        jobs.append((copy, rows, here, out))
    load()
    low = low_ref[...].astype(jnp.bfloat16)
    total = jnp.zeros((low.shape[0], LANES), jnp.float32)
    for copy, rows, here, out in jobs:
        copy.wait()
        part = lax.dot_general(low, slab_v[here], ROWS, preferred_element_type=jnp.float32)
        out[...] = part
        part = part * cell_ref[:, rows]
        for j in range(0, width, LANES):
            total += part[:, j : j + LANES]
    return total


def copies(pairs, sem):
    moves = [pltpu.make_async_copy(a, b, sem.at[i]) for i, (a, b) in enumerate(pairs)]
    for move in moves:
        move.start()
    return lambda: [move.wait() for move in moves]


def pass_one_a(n_rel, chan_hbm, cell_hbm, slab_hbm, send_ref, keep_ref, rhs_ref, slab_v, chan_ref, cell_ref, sem, small_sem):
    load = copies([(chan_hbm, chan_ref), (cell_hbm, cell_ref)], small_sem)
    rhs_ref[...] = multiply(0, n_rel, chan_ref, cell_ref, slab_hbm, slab_v, sem, send_ref, keep_ref, load)


def pass_one_b(
    start, all_rows, all_cols, n_cell, n_chan, chan_hbm, cell_hbm, slab_hbm, rhs_in_ref, after_hbm,
    send_ref, keep_ref, stats_ref, slab_v, chan_ref, cell_ref, sem, small_sem,
):
    del after_hbm
    n_rel = n_chan // 2
    load = copies([(chan_hbm, chan_ref), (cell_hbm, cell_ref)], small_sem)
    total = multiply(start, n_rel, chan_ref, cell_ref, slab_hbm, slab_v, sem, send_ref, keep_ref, load)
    chan, cell = chan_ref[...], cell_ref[...]
    chan_gram = lax.dot_general(chan, chan, ROWS, precision=HI) / (all_cols * n_cell)
    cell_gram = lax.dot_general(cell, cell, ROWS, precision=HI) / (all_rows * n_chan)
    total = total + rhs_in_ref[...]
    rhs = jnp.sum(total, axis=1, keepdims=True) / math.sqrt(all_rows * all_cols)
    pad = jnp.zeros((chan.shape[0], LANES - 1 - 2 * chan.shape[0]), jnp.float32)
    stats_ref[...] = jnp.concatenate([cell_gram, chan_gram, rhs, pad], axis=1)


def solve_one(stats_ref, acc_ref, row_ref, gram_ref, out_ref):
    stats = stats_ref[...]
    n = stats.shape[0]
    cell_norm, chan_norm, rhs = stats[:, :n], stats[:, n : 2 * n], stats[:, 2 * n : 2 * n + 1]
    time = eliminate(jnp.concatenate([cell_norm * chan_norm, rhs], axis=1), n)
    row = jnp.sum(eye(n) * time, axis=0, keepdims=True)
    outer = time * row
    gram = acc_ref[...] + chan_norm * outer
    inverse = eliminate(jnp.concatenate([gram, eye(n)], axis=1), n)
    row_ref[...] = row
    gram_ref[...] = gram
    pad = jnp.zeros((n, LANES - 2 * n - 1), jnp.float32)
    out_ref[...] = jnp.concatenate([inverse, outer, time, pad], axis=1)


def pass_two(all_rows, all_cols, where, n_rel, resume, solved_ref, mttkrp_ref, *refs):
    slabs, refs = refs[:CHUNKS], refs[CHUNKS:]
    pieces, refs = refs[: len(where)], refs[len(where) :]
    before, refs = (refs[:3], refs[3:]) if resume else (None, refs)
    mttkrp_hbm, factor_hbm, out_ref, mttkrp_v, factor_v, sem = refs
    n = solved_ref.shape[0]
    cols = slabs[0].shape[1]
    inverse = solved_ref[:, :n]
    time = solved_ref[:, 2 * n : 2 * n + 1] / math.sqrt(all_cols)
    total = before[2][:, :cols] if resume else jnp.zeros((n, cols), jnp.float32)
    gram = before[2][:, cols : cols + n] if resume else jnp.zeros((n, n), jnp.float32)
    moves = []
    for i, ((chunk, rel), piece) in enumerate(zip(where, pieces)):
        width = piece.shape[1]
        at = place(rel, n_rel, width)
        rows = pl.ds(pl.multiple_of(chunk * n_rel * width + at, width), width)
        right = mttkrp_ref[:, rows] + time * piece[...]
        mttkrp_v[i] = right
        factor = jnp.dot(inverse, right, precision=HI)
        factor_v[i] = factor
        for a, b in ((mttkrp_v, mttkrp_hbm), (factor_v, factor_hbm)):
            moves.append(pltpu.make_async_copy(a.at[i], b.at[:, rows], sem.at[len(moves)]))
            moves[-1].start()
        gram += lax.dot_general(factor, factor, ROWS, precision=HI) / all_rows
        low = factor.astype(jnp.bfloat16)
        total += jnp.dot(low, slabs[chunk][pl.ds(at, width)], preferred_element_type=jnp.float32)
    out_ref[:, :cols] = total
    out_ref[:, cols:] = jnp.concatenate([gram, jnp.zeros((n, LANES - n), jnp.float32)], axis=1)
    for move in moves:
        move.wait()


def solve_two(all_rows, n_parts, solved_ref, mttkrp_ref, acc_ref, *refs):
    parts = [r[...] for r in refs[:n_parts]]
    new_mttkrp, new_factor, new_gram = refs[n_parts:]
    while len(parts) > 1:
        parts = [a + b for a, b in zip(parts[::2], parts[1::2])]
    (summed,) = parts
    n, cols = mttkrp_ref.shape
    outer = solved_ref[:, n : 2 * n]
    time = solved_ref[:, 2 * n : 2 * n + 1] / math.sqrt(all_rows)
    gram = acc_ref[...] + summed[:, cols : cols + n] * outer
    inverse = eliminate(jnp.concatenate([gram, eye(n)], axis=1), n)
    right = mttkrp_ref[...] + time * summed[:, :cols]
    new_mttkrp[...] = right
    new_factor[...] = jnp.dot(inverse, right, precision=HI)
    new_gram[...] = gram


def over_cell(x, n_cell):
    masks = 1
    while masks < n_cell // 4:
        masks *= 2
        x = x + lax.ppermute(x, "cell", [(i, i ^ (2 * masks)) for i in range(n_cell)])
    near = [m for m in (1, 2, 3) if m < n_cell]
    return [x] + [lax.ppermute(x, "cell", [(i, i ^ m) for i in range(n_cell)]) for m in near]


def pair_sum(parts):
    while len(parts) > 1:
        parts = [a + b for a, b in zip(parts[::2], parts[1::2])]
    return parts[0]


def trade(x, mask, n_chan):
    return lax.ppermute(x, "chan", [(i, i ^ mask) for i in range(n_chan)])


def over_chan(x, n_chan):
    width = x.shape[1] // (n_chan // 4)
    mask = 2
    while mask < n_chan // 2:
        blocks = [x[:, i : i + width] for i in range(0, x.shape[1], width)]
        keep, send = (jnp.concatenate(b, axis=1) if len(b) > 1 else b[0] for b in (blocks[::2], blocks[1::2]))
        x = keep + trade(send, mask, n_chan)
        mask *= 2
    have = {0: x + trade(x, mask, n_chan)}
    while mask > 2:
        mask //= 2
        have.update({rel + mask: trade(block, mask, n_chan) for rel, block in list(have.items())})
    have.update({rel + 1: trade(block, 1, n_chan) for rel, block in list(have.items())})
    return have


def body(slab, cell_factor, chan_factor, cell_mttkrp, chan_mttkrp, cell_gram_acc, chan_gram_acc):
    n_cell = lax.axis_size("cell")
    n_chan = lax.axis_size("chan")
    rows, cols = slab.shape
    rank = cell_factor.shape[0]
    all_rows, all_cols = rows * n_cell, cols * n_chan
    n_rel = n_chan // 2
    start = rows // CHUNKS
    width = start // n_rel
    f32 = functools.partial(jax.ShapeDtypeStruct, dtype=jnp.float32)
    hbm = pl.BlockSpec(memory_space=pltpu.HBM)
    inputs = [pltpu.with_memory_space_constraint(x, pltpu.HBM) for x in (chan_factor, cell_factor, slab)]
    half = f32((rank, start // 2))
    tile = f32((rank, LANES))
    slab_half = pltpu.VMEM((start, cols), slab.dtype)
    scratch = [
        pltpu.VMEM(chan_factor.shape, jnp.float32),
        pltpu.VMEM(cell_factor.shape, jnp.float32),
        pltpu.SemaphoreType.DMA((n_rel,)),
        pltpu.SemaphoreType.DMA((2,)),
    ]

    send, keep, rhs, slab_a = pl.pallas_call(
        functools.partial(pass_one_a, n_rel),
        in_specs=[hbm] * 3,
        out_specs=[WHOLE] * 4,
        out_shape=[half, half, tile, slab_half],
        scratch_shapes=scratch,
        compiler_params=PARAMS,
        cost_estimate=cost(4.5),
        name="pass_one_a",
    )(*inputs)
    chip_a = keep + trade(send, 1, n_chan)
    send, keep, stats, slab_b = pl.pallas_call(
        functools.partial(pass_one_b, start, all_rows, all_cols, n_cell, n_chan),
        in_specs=[hbm] * 3 + [WHOLE, pl.BlockSpec(memory_space=pl.ANY)],
        out_specs=[WHOLE] * 4,
        out_shape=[half, half, tile, slab_half],
        scratch_shapes=scratch,
        compiler_params=PARAMS,
        cost_estimate=cost(6),
        name="pass_one_b",
    )(*inputs, rhs, chip_a)
    chip_b = keep + trade(send, 1, n_chan)
    slabs = [pltpu.with_memory_space_constraint(x, pltpu.VMEM) for x in (slab_a, slab_b)]
    blocks_a, blocks_b = over_chan(chip_a, n_chan), over_chan(chip_b, n_chan)

    stats = pair_sum(over_cell(stats, n_cell))
    mask = 1
    while mask < n_chan:
        stats = stats + trade(stats, mask, n_chan)
        mask *= 2
    row, new_cell_gram, solved = pl.pallas_call(
        solve_one,
        in_specs=[WHOLE] * 2,
        out_specs=[WHOLE] * 3,
        out_shape=[f32((1, rank)), f32((rank, rank)), tile],
        compiler_params=SMALL,
        cost_estimate=cost(5.8),
        name="solve_one",
    )(stats, cell_gram_acc)

    late = [rel for rel in blocks_b if rel & 2]
    calls = [
        [((0, rel), x) for rel, x in blocks_a.items()] + [((1, rel), x) for rel, x in blocks_b.items() if rel not in late],
        [((1, rel), blocks_b[rel]) for rel in late],
    ]
    state = []
    for blocks in calls:
        where, pieces = zip(*blocks)
        n_in = 2 + CHUNKS + len(where)
        state = pl.pallas_call(
            functools.partial(pass_two, all_rows, all_cols, where, n_rel, bool(state)),
            in_specs=[WHOLE] * n_in + ([hbm, hbm, WHOLE] if state else []),
            out_specs=[hbm, hbm, WHOLE],
            out_shape=[f32((rank, rows)), f32((rank, rows)), f32((rank, cols + LANES))],
            scratch_shapes=[pltpu.VMEM((len(where), rank, width), jnp.float32)] * 2
            + [pltpu.SemaphoreType.DMA((2 * len(where),))],
            input_output_aliases={n_in: 0, n_in + 1: 1} if state else {},
            compiler_params=PARAMS,
            cost_estimate=cost(0.6 * len(where)),
            name="pass_two_b" if state else "pass_two_a",
        )(solved, cell_mttkrp, *slabs, *pieces, *state)
    new_cell_mttkrp, new_cell_factor, part = state

    parts = over_cell(part, n_cell)
    new_chan_mttkrp, new_chan_factor, new_chan_gram = pl.pallas_call(
        functools.partial(solve_two, all_rows, len(parts)),
        in_specs=[WHOLE] * (3 + len(parts)),
        out_specs=[WHOLE] * 3,
        out_shape=[f32((rank, cols)), f32((rank, cols)), f32((rank, rank))],
        compiler_params=SMALL,
        cost_estimate=cost(3.7),
        name="solve_two",
    )(solved, chan_mttkrp, chan_gram_acc, *parts)
    return (
        row.reshape(rank),
        new_cell_factor,
        new_chan_factor,
        new_cell_mttkrp,
        new_chan_mttkrp,
        new_cell_gram,
        new_chan_gram,
    )


def solution(mesh):
    placed = (
        P("cell", "chan"),
        P(None, "cell"),
        P(None, "chan"),
        P(None, "cell"),
        P(None, "chan"),
        P(),
        P(),
    )
    return jax.shard_map(
        body,
        mesh=mesh,
        in_specs=placed,
        out_specs=(
            P(),
            P(None, "cell"),
            P(None, "chan"),
            P(None, "cell"),
            P(None, "chan"),
            P(),
            P(),
        ),
        check_vma=False,
    )
```

```python
import functools
import math

import jax
import jax.numpy as jnp
from jax import lax
from jax.experimental import pallas as pl
from jax.experimental.pallas import tpu as pltpu
from jax.sharding import PartitionSpec as P

CHUNKS = 2
LANES = 128
HI = lax.Precision.HIGHEST
ROWS = (((1,), (1,)), ((), ()))
WHOLE = pl.BlockSpec(memory_space=pltpu.VMEM)
PARAMS = pltpu.CompilerParams(vmem_limit_bytes=12 << 20)


def cost(us):
    return pl.CostEstimate(flops=int(us * 1e9), bytes_accessed=int(us * 3e6), transcendentals=0)


SMALL = pltpu.CompilerParams(vmem_limit_bytes=4 << 20)


def eye(n):
    i = lax.broadcasted_iota(jnp.int32, (n, n), 0)
    j = lax.broadcasted_iota(jnp.int32, (n, n), 1)
    return (i == j).astype(jnp.float32)


def eliminate(matrix, right):
    n = matrix.shape[0]
    rows = lax.broadcasted_iota(jnp.int32, (n, LANES), 0)
    spread = [jnp.broadcast_to(matrix[:, k : k + 1], (n, LANES)) for k in range(n)]
    right = jnp.concatenate([right, jnp.zeros((n, LANES - right.shape[1]), jnp.float32)], axis=1)
    for k in range(n):
        column = spread[k]
        scale = 1.0 / column[k : k + 1, :]
        at_k = rows == k

        def clear(x):
            row = x[k : k + 1, :] * scale
            return jnp.where(at_k, row, x - column * row)

        spread[k + 1 :] = [clear(x) for x in spread[k + 1 :]]
        right = clear(right)
    return right


def gram(x):
    high = x.astype(jnp.bfloat16)
    low = (x - high.astype(jnp.float32)).astype(jnp.bfloat16)
    dot = functools.partial(lax.dot_general, dimension_numbers=ROWS, preferred_element_type=jnp.float32)
    cross = dot(high, low)
    return dot(high, high) + (cross + cross.T)


def place(rel, n_rel, width):
    me = lax.rem(lax.axis_index("chan"), n_rel)
    return pl.multiple_of(lax.bitwise_xor(me, rel) * width, width)


def multiply(start, n_rel, low_ref, cell_ref, slab_hbm, slab_v, sem, send_ref, keep_ref, load):
    width = slab_v.shape[0] // n_rel
    jobs = []
    for rel in [*range(1, n_rel, 2), *range(0, n_rel, 2)]:
        at = place(rel, n_rel, width)
        rows = pl.ds(pl.multiple_of(start + at, width), width)
        here = pl.ds(at, width)
        copy = pltpu.make_async_copy(slab_hbm.at[rows], slab_v.at[here], sem.at[len(jobs)])
        copy.start()
        out = (send_ref if rel % 2 else keep_ref).at[:, pl.ds(rel // 2 * width, width)]
        jobs.append((copy, rows, here, out))
    load()
    low = low_ref[...].astype(jnp.bfloat16)
    total = jnp.zeros((low.shape[0], LANES), jnp.float32)
    for copy, rows, here, out in jobs:
        copy.wait()
        part = lax.dot_general(low, slab_v[here], ROWS, preferred_element_type=jnp.float32)
        out[...] = part
        part = part * cell_ref[:, rows]
        for j in range(0, width, LANES):
            total += part[:, j : j + LANES]
    return total


def copies(pairs, sem):
    moves = [pltpu.make_async_copy(a, b, sem.at[i]) for i, (a, b) in enumerate(pairs)]
    for move in moves:
        move.start()
    return lambda: [move.wait() for move in moves]


def pass_one_a(n_rel, chan_hbm, cell_hbm, slab_hbm, send_ref, keep_ref, rhs_ref, slab_v, chan_ref, cell_ref, sem, small_sem):
    load = copies([(chan_hbm, chan_ref), (cell_hbm, cell_ref)], small_sem)
    rhs_ref[...] = multiply(0, n_rel, chan_ref, cell_ref, slab_hbm, slab_v, sem, send_ref, keep_ref, load)


def pass_one_b(
    start, all_rows, all_cols, n_cell, n_chan, chan_hbm, cell_hbm, slab_hbm, rhs_in_ref, after_hbm,
    send_ref, keep_ref, stats_ref, slab_v, chan_ref, cell_ref, sem, small_sem,
):
    del after_hbm
    n_rel = n_chan // 2
    load = copies([(chan_hbm, chan_ref), (cell_hbm, cell_ref)], small_sem)
    total = multiply(start, n_rel, chan_ref, cell_ref, slab_hbm, slab_v, sem, send_ref, keep_ref, load)
    chan, cell = chan_ref[...], cell_ref[...]
    chan_gram = gram(chan) / (all_cols * n_cell)
    cell_gram = gram(cell) / (all_rows * n_chan)
    total = total + rhs_in_ref[...]
    rhs = jnp.sum(total, axis=1, keepdims=True) / math.sqrt(all_rows * all_cols)
    pad = jnp.zeros((chan.shape[0], LANES - 1 - 2 * chan.shape[0]), jnp.float32)
    stats_ref[...] = jnp.concatenate([cell_gram, chan_gram, rhs, pad], axis=1)


def solve_one(stats_ref, acc_ref, row_ref, gram_ref, out_ref):
    stats = stats_ref[...]
    n = stats.shape[0]
    cell_norm, chan_norm, rhs = stats[:, :n], stats[:, n : 2 * n], stats[:, 2 * n : 2 * n + 1]
    time = eliminate(cell_norm * chan_norm, rhs)[:, :1]
    row = jnp.sum(eye(n) * time, axis=0, keepdims=True)
    outer = time * row
    gram = acc_ref[...] + chan_norm * outer
    inverse = eliminate(gram, eye(n))[:, :n]
    row_ref[...] = row
    gram_ref[...] = gram
    pad = jnp.zeros((n, LANES - 2 * n - 1), jnp.float32)
    out_ref[...] = jnp.concatenate([inverse, outer, time, pad], axis=1)


def pass_two(all_rows, all_cols, where, n_rel, resume, solved_ref, mttkrp_ref, *refs):
    slabs, refs = refs[:CHUNKS], refs[CHUNKS:]
    pieces, refs = refs[: len(where)], refs[len(where) :]
    before, refs = (refs[:3], refs[3:]) if resume else (None, refs)
    mttkrp_hbm, factor_hbm, out_ref, mttkrp_v, factor_v, sem = refs
    n = solved_ref.shape[0]
    cols = slabs[0].shape[1]
    inverse = solved_ref[:, :n]
    time = solved_ref[:, 2 * n : 2 * n + 1] / math.sqrt(all_cols)
    total = before[2][:, :cols] if resume else jnp.zeros((n, cols), jnp.float32)
    total_gram = before[2][:, cols : cols + n] if resume else jnp.zeros((n, n), jnp.float32)
    moves = []
    for i, ((chunk, rel), piece) in enumerate(zip(where, pieces)):
        width = piece.shape[1]
        at = place(rel, n_rel, width)
        rows = pl.ds(pl.multiple_of(chunk * n_rel * width + at, width), width)
        right = mttkrp_ref[:, rows] + time * piece[...]
        mttkrp_v[i] = right
        factor = jnp.dot(inverse, right, precision=HI)
        factor_v[i] = factor
        for a, b in ((mttkrp_v, mttkrp_hbm), (factor_v, factor_hbm)):
            moves.append(pltpu.make_async_copy(a.at[i], b.at[:, rows], sem.at[len(moves)]))
            moves[-1].start()
        total_gram += lax.dot_general(factor, factor, ROWS, precision=HI) / all_rows
        low = factor.astype(jnp.bfloat16)
        total += jnp.dot(low, slabs[chunk][pl.ds(at, width)], preferred_element_type=jnp.float32)
    out_ref[:, :cols] = total
    out_ref[:, cols:] = jnp.concatenate([total_gram, jnp.zeros((n, LANES - n), jnp.float32)], axis=1)
    for move in moves:
        move.wait()


def solve_two(all_rows, n_parts, solved_ref, mttkrp_ref, acc_ref, *refs):
    parts = [r[...] for r in refs[:n_parts]]
    new_mttkrp, new_factor, new_gram = refs[n_parts:]
    while len(parts) > 1:
        parts = [a + b for a, b in zip(parts[::2], parts[1::2])]
    (summed,) = parts
    n, cols = mttkrp_ref.shape
    outer = solved_ref[:, n : 2 * n]
    time = solved_ref[:, 2 * n : 2 * n + 1] / math.sqrt(all_rows)
    gram = acc_ref[...] + summed[:, cols : cols + n] * outer
    inverse = eliminate(gram, eye(n))[:, :n]
    right = mttkrp_ref[...] + time * summed[:, :cols]
    new_mttkrp[...] = right
    new_factor[...] = jnp.dot(inverse, right, precision=HI)
    new_gram[...] = gram


def over_cell(x, n_cell):
    masks = 1
    while masks < n_cell // 4:
        masks *= 2
        x = x + lax.ppermute(x, "cell", [(i, i ^ (2 * masks)) for i in range(n_cell)])
    near = [m for m in (1, 2, 3) if m < n_cell]
    return [x] + [lax.ppermute(x, "cell", [(i, i ^ m) for i in range(n_cell)]) for m in near]


def pair_sum(parts):
    while len(parts) > 1:
        parts = [a + b for a, b in zip(parts[::2], parts[1::2])]
    return parts[0]


def trade(x, mask, n_chan):
    return lax.ppermute(x, "chan", [(i, i ^ mask) for i in range(n_chan)])


def after(x, others):
    return lax.optimization_barrier((x, others))[0]


def halve(x, n_chan):
    width = x.shape[1] // (n_chan // 4)
    mask = 2
    while mask < n_chan // 2:
        blocks = [x[:, i : i + width] for i in range(0, x.shape[1], width)]
        keep, send = (jnp.concatenate(b, axis=1) if len(b) > 1 else b[0] for b in (blocks[::2], blocks[1::2]))
        x = keep + trade(send, mask, n_chan)
        mask *= 2
    return x


def give_back(x, n_chan):
    have = {0: x}
    mask = n_chan // 2
    while mask > 2:
        mask //= 2
        have.update({rel + mask: trade(block, mask, n_chan) for rel, block in list(have.items())})
    have.update({rel + 1: trade(block, 1, n_chan) for rel, block in list(have.items())})
    return have


def body(slab, cell_factor, chan_factor, cell_mttkrp, chan_mttkrp, cell_gram_acc, chan_gram_acc):
    n_cell = lax.axis_size("cell")
    n_chan = lax.axis_size("chan")
    rows, cols = slab.shape
    rank = cell_factor.shape[0]
    all_rows, all_cols = rows * n_cell, cols * n_chan
    n_rel = n_chan // 2
    start = rows // CHUNKS
    width = start // n_rel
    f32 = functools.partial(jax.ShapeDtypeStruct, dtype=jnp.float32)
    hbm = pl.BlockSpec(memory_space=pltpu.HBM)
    inputs = [pltpu.with_memory_space_constraint(x, pltpu.HBM) for x in (chan_factor, cell_factor, slab)]
    half = f32((rank, start // 2))
    tile = f32((rank, LANES))
    slab_half = pltpu.VMEM((start, cols), slab.dtype)
    scratch = [
        pltpu.VMEM(chan_factor.shape, jnp.float32),
        pltpu.VMEM(cell_factor.shape, jnp.float32),
        pltpu.SemaphoreType.DMA((n_rel,)),
        pltpu.SemaphoreType.DMA((2,)),
    ]

    send, keep, rhs, slab_a = pl.pallas_call(
        functools.partial(pass_one_a, n_rel),
        in_specs=[hbm] * 3,
        out_specs=[WHOLE] * 4,
        out_shape=[half, half, tile, slab_half],
        scratch_shapes=scratch,
        compiler_params=PARAMS,
        cost_estimate=cost(4.5),
        name="pass_one_a",
    )(*inputs)
    chip_a = keep + trade(send, 1, n_chan)
    send, keep, stats, slab_b = pl.pallas_call(
        functools.partial(pass_one_b, start, all_rows, all_cols, n_cell, n_chan),
        in_specs=[hbm] * 3 + [WHOLE, pl.BlockSpec(memory_space=pl.ANY)],
        out_specs=[WHOLE] * 4,
        out_shape=[half, half, tile, slab_half],
        scratch_shapes=scratch,
        compiler_params=PARAMS,
        cost_estimate=cost(12),
        name="pass_one_b",
    )(*inputs, rhs, chip_a)
    chip_b = keep + trade(send, 1, n_chan)
    slabs = [pltpu.with_memory_space_constraint(x, pltpu.VMEM) for x in (slab_a, slab_b)]
    ready_a, ready_b = halve(chip_a, n_chan), halve(chip_b, n_chan)
    last = n_chan // 2
    stats = after(stats, (ready_a, chip_b))
    stats = pair_sum(over_cell(stats, n_cell))
    total_a = ready_a + trade(ready_a, last, n_chan)
    mask = 1
    while mask < n_chan:
        stats = stats + trade(stats, mask, n_chan)
        mask *= 2
    total_b = ready_b + trade(ready_b, last, n_chan)
    blocks_a, blocks_b = give_back(total_a, n_chan), give_back(total_b, n_chan)
    row, new_cell_gram, solved = pl.pallas_call(
        solve_one,
        in_specs=[WHOLE] * 2,
        out_specs=[WHOLE] * 3,
        out_shape=[f32((1, rank)), f32((rank, rank)), tile],
        compiler_params=SMALL,
        cost_estimate=cost(5.8),
        name="solve_one",
    )(stats, cell_gram_acc)

    late = [rel for rel in blocks_b if rel & 2]
    calls = [
        [((0, rel), x) for rel, x in blocks_a.items()] + [((1, rel), x) for rel, x in blocks_b.items() if rel not in late],
        [((1, rel), blocks_b[rel]) for rel in late],
    ]
    state = []
    for blocks in calls:
        where, pieces = zip(*blocks)
        n_in = 2 + CHUNKS + len(where)
        state = pl.pallas_call(
            functools.partial(pass_two, all_rows, all_cols, where, n_rel, bool(state)),
            in_specs=[WHOLE] * n_in + ([hbm, hbm, WHOLE] if state else []),
            out_specs=[hbm, hbm, WHOLE],
            out_shape=[f32((rank, rows)), f32((rank, rows)), f32((rank, cols + LANES))],
            scratch_shapes=[pltpu.VMEM((len(where), rank, width), jnp.float32)] * 2
            + [pltpu.SemaphoreType.DMA((2 * len(where),))],
            input_output_aliases={n_in: 0, n_in + 1: 1} if state else {},
            compiler_params=PARAMS,
            cost_estimate=cost(0.6 * len(where)),
            name="pass_two_b" if state else "pass_two_a",
        )(solved, cell_mttkrp, *slabs, *pieces, *state)
    new_cell_mttkrp, new_cell_factor, part = state

    parts = over_cell(part, n_cell)
    new_chan_mttkrp, new_chan_factor, new_chan_gram = pl.pallas_call(
        functools.partial(solve_two, all_rows, len(parts)),
        in_specs=[WHOLE] * (3 + len(parts)),
        out_specs=[WHOLE] * 3,
        out_shape=[f32((rank, cols)), f32((rank, cols)), f32((rank, rank))],
        compiler_params=SMALL,
        cost_estimate=cost(3.7),
        name="solve_two",
    )(solved, chan_mttkrp, chan_gram_acc, *parts)
    return (
        row.reshape(rank),
        new_cell_factor,
        new_chan_factor,
        new_cell_mttkrp,
        new_chan_mttkrp,
        new_cell_gram,
        new_chan_gram,
    )


def solution(mesh):
    placed = (
        P("cell", "chan"),
        P(None, "cell"),
        P(None, "chan"),
        P(None, "cell"),
        P(None, "chan"),
        P(),
        P(),
    )
    return jax.shard_map(
        body,
        mesh=mesh,
        in_specs=placed,
        out_specs=(
            P(),
            P(None, "cell"),
            P(None, "chan"),
            P(None, "cell"),
            P(None, "chan"),
            P(),
            P(),
        ),
        check_vma=False,
    )
```
